32 devices in a mesh: group: 2 (over y), tm: 4 (over x, core), inst: 4 (over z).
Axes of the slice: x: 2, y: 2, z: 4, core: 2. Of those that a mesh axis runs over, the one named last changes fastest.
Arguments:
- quotes: float32 [8, 16384], P(('group', 'tm'), 'inst'), parts along dimension 0, may hold values from -6 to 6
- present: int32 [8, 16384], P(('group', 'tm'), 'inst'), parts along dimension 0, may hold values from 0 to 1
- loadings: bfloat16 [16384, 512], P('inst'), may hold values from -0.07 to 0.07
- noise_var: float32 [16384], P('inst'), may hold values from 0.5 to 4
- persistence: float32 [512], replicated, may hold values from 0.2 to 0.99
- shock_var: float32 [512], replicated, may hold values from 0.05 to 0.5
Outputs:
- filtered_mean: float32 [8, 512], P(('group', 'tm')), parts along dimension 0
- filtered_var: float32 [8, 512], P(('group', 'tm')), parts along dimension 0
- smoothed_mean: float32 [8, 512], P(('group', 'tm')), parts along dimension 0
The draws below stay inside these ranges and needn't reach their ends.
There are 2 independent parts, one for each index of `group`. The reference program is written for one: setup_inputs(seed, part) draws one part's arguments, and reference() takes and returns one part's arrays. A program takes and returns all parts, laid end to end along the dimension named above; an argument that names none is the same for every part. Nothing has to cross between parts.
All inputs are finite; a program needn't handle non-finite values.
Results may differ from the reference program's by a relative error of at most 0.0027.
Values sent between devices are 32-bit elements; how exact they have to be, the bound alone decides.
A program may use at most 128 MiB of HBM per device.

```python
import math
import jax
import jax.numpy as jnp
from jax import lax

FACTORS = 512
INST = 16384
STEPS = 4


sector_count = 16


def draw_present(key, part):
    on_key = jax.random.fold_in(key, 101)
    inside_key = jax.random.fold_in(key, 102)
    sector_on = jax.random.randint(on_key, (STEPS, sector_count), 0, 2)
    inside = (jax.random.randint(inside_key, (STEPS, INST), 0, 8) < 7).astype(jnp.int32)
    sector_of = jnp.arange(INST) % sector_count
    return (sector_on[:, sector_of] * inside).astype(jnp.int32)


def draw_loadings(key, part):
    idio_key = jax.random.fold_in(key, 201)
    strength_key = jax.random.fold_in(key, 202)
    vector_key = jax.random.fold_in(key, 203)
    idio = jnp.clip(jax.random.normal(idio_key, (INST, FACTORS), jnp.float32), -4.0, 4.0)
    strength = jnp.clip(jax.random.normal(strength_key, (INST,), jnp.float32), -4.0, 4.0)
    vectors = jnp.clip(jax.random.normal(vector_key, (sector_count, FACTORS), jnp.float32), -4.0, 4.0)
    sector_of = jnp.arange(INST) % sector_count
    common = strength[:, None] * vectors[sector_of]
    values = (0.3 * idio + 2.0 * common) * (1.0 / math.sqrt(INST))
    return jnp.clip(values, -0.07, 0.07).astype(jnp.bfloat16)


def shard_levels(stream_key, extent, shards, least, high):
    gain, own = 1.0, jax.random.fold_in(stream_key, 6)
    for axis_at, blocks in shards:
        heights = jnp.exp(jax.random.uniform(jax.random.fold_in(own, axis_at), (blocks,), jnp.float32, least / len(shards), high / len(shards)))
        gain = gain * jnp.repeat(heights, extent[axis_at] // blocks).reshape([-1 if axis == axis_at else 1 for axis in range(len(extent))])
    return gain


def scatter_about(own_key, dims, scale, most, pieces=(), held_as=jnp.bfloat16):
    entries = jax.random.normal(own_key, dims, jnp.float32) * scale
    if len(pieces) > 0:
        entries = shard_levels(own_key, dims, pieces, -0.22, 0.18) * entries
    return jnp.clip(entries, min=-most, max=most).astype(held_as)


def setup_inputs(seed: int = 0, part: int = 0) -> dict:
    key_of = jax.random.split(jax.random.key(seed), 7)
    own_keys = jax.random.split(jax.random.fold_in(key_of[6], part), 7)
    return {
        "quotes": scatter_about(own_keys[0], (STEPS, INST), 1.0, 6.0, ((0, 4), (1, 4)), jnp.float32),
        "present": draw_present(jax.random.fold_in(jax.random.fold_in(key_of[6], part), 71), part),
        "loadings": draw_loadings(jax.random.fold_in(key_of[6], 71), part),
        "noise_var": jnp.clip(jnp.exp(math.log(4.0) - 2.0794415 * jax.random.uniform(key_of[3], (INST,), jnp.float32) ** shard_levels(key_of[3], (INST,), ((0, 4),), -0.2, 0.2)), 0.5, 4.0),
        "persistence": jnp.clip(jax.random.uniform(key_of[4], (FACTORS,), jnp.float32, 0.2, 0.99), 0.2, 0.99),
        "shock_var": jnp.clip(jnp.exp(jax.random.uniform(key_of[5], (FACTORS,), jnp.float32, math.log(0.05), math.log(0.5))), 0.05, 0.5),
    }


highest = lax.Precision.HIGHEST

def step_information(loadings, noise_var, row_quotes, row_present):
    scaled = row_present.astype(jnp.float32) / noise_var
    weighted = (loadings.astype(jnp.float32) * scaled[:, None]).astype(jnp.bfloat16)
    info_matrix = lax.dot_general(weighted.astype(jnp.float32), loadings.astype(jnp.float32), (((0,), (0,)), ((), ())), preferred_element_type=jnp.float32)
    info_vector = jnp.dot(row_quotes, weighted.astype(jnp.float32), precision=highest)
    return (info_matrix, info_vector)

def reference(quotes, present, loadings, noise_var, persistence, shock_var):
    factors = loadings.shape[1]
    identity_matrix = jnp.eye(factors, dtype=jnp.float32)

    def gather_step(inputs):
        return step_information(loadings, noise_var, inputs[0], inputs[1])
    info_matrix, info_vector = lax.map(gather_step, (quotes, present))

    def forward(carried_state, inputs):
        prior_mean, prior_cov = carried_state
        pred_mean = persistence * prior_mean
        pred_cov = persistence[:, None] * prior_cov * persistence[None, :] + jnp.diag(shock_var)
        pred_prec = jnp.linalg.solve(pred_cov, identity_matrix)
        post_cov = jnp.linalg.solve(pred_prec + inputs[0], identity_matrix)
        post_mean = jnp.dot(post_cov, jnp.dot(pred_prec, pred_mean, precision=highest) + inputs[1], precision=highest)
        return ((post_mean, post_cov), (post_mean, post_cov))
    initial = (jnp.zeros((factors,), jnp.float32), jnp.zeros((factors, factors), jnp.float32))
    _, (means, covs) = lax.scan(forward, initial, (info_matrix, info_vector))

    def backward(next_value, inputs):
        mean_now, cov_now = inputs
        pred_cov = persistence[:, None] * cov_now * persistence[None, :] + jnp.diag(shock_var)
        smoother_gain = jnp.linalg.solve(pred_cov, persistence[:, None] * cov_now.T).T
        smoothed = mean_now + jnp.dot(smoother_gain, next_value - persistence * mean_now, precision=highest)
        return (smoothed, smoothed)
    _, earlier_values = lax.scan(backward, means[-1], (means[:-1], covs[:-1]), reverse=True)
    smoothed_mean = jnp.concatenate([earlier_values, means[-1:]], axis=0)
    filtered_var = jnp.diagonal(covs, axis1=1, axis2=2)
    return (means, filtered_var, smoothed_mean)
```

```python
import functools

import jax
import jax.numpy as jnp
from jax import lax
from jax.experimental import pallas as pl
from jax.experimental.pallas import tpu as pltpu
from jax.sharding import PartitionSpec as P

f32 = jnp.float32
bf16 = jnp.bfloat16
highest = lax.Precision.HIGHEST


def mm(left, right):
    return jnp.dot(left, right, preferred_element_type=f32)


def mm_full(left, right):
    return jnp.dot(left, right, precision=highest, preferred_element_type=f32)


def eye_mask(size):
    rows = lax.broadcasted_iota(jnp.int32, (size, size), 0)
    columns = lax.broadcasted_iota(jnp.int32, (size, size), 1)
    return rows == columns


def vec_mat(vector, matrix):
    high = vector.astype(bf16).astype(f32)
    low = vector - high
    index = lax.broadcasted_iota(jnp.int32, (16, vector.shape[1]), 0)
    rows = jnp.where(index == 0, high, jnp.where(index == 1, low, 0.0)).astype(bf16)
    m_high = matrix.astype(bf16)
    m_low = (matrix - m_high.astype(f32)).astype(bf16)
    return jnp.sum(mm(rows, m_high) + mm(rows, m_low), axis=0, keepdims=True)


def inverse(a_ref, x_ref, e_ref, ah_ref, al_ref, r_ref):
    size = a_ref.shape[0]
    a = a_ref[...]
    ah = a.astype(bf16)
    ah_ref[...] = ah
    al_ref[...] = (a - ah.astype(f32)).astype(bf16)
    square = mm(ah, ah)
    fourth = jnp.full((8, 128), jnp.sum(square * square), f32)
    upper = jnp.maximum(jnp.sqrt(jnp.sqrt(fourth)) * 1.01, 1.5)
    lower = 0.98
    slope = 2.0 / (upper - lower)
    centre = (upper + lower) / (upper - lower)
    height = 1.0 / ((4.0 * centre * centre - 3.0) * centre)
    c0 = (12.0 * centre * centre - 3.0) * slope * height
    c1 = -12.0 * centre * slope * slope * height
    c2 = 4.0 * slope * slope * slope * height
    ident = jnp.where(eye_mask(size), f32(1.0), f32(0.0))
    x_ref[...] = c0[:1, :1] * ident + c1[:1, :1] * a_ref[...] + c2[:1, :1] * square
    r_ref[...] = height
    count = jnp.zeros((8, 128), f32)
    rate = height
    for _ in range(12):
        count = count + jnp.where(rate > 0.02, 1.0, 0.0)
        rate = rate * rate / (2.0 - rate * rate)
    steps = jnp.max(count).astype(jnp.int32)

    def newton(_, carry):
        rate = r_ref[...]
        r_ref[...] = rate * rate / (2.0 - rate * rate)
        weight = (2.0 / (2.0 - rate * rate))[:1, :1]
        xh = x_ref[...].astype(bf16)
        ident = jnp.where(eye_mask(size), f32(1.0), f32(0.0))
        e = (ident - mm(ah_ref[...], xh)).astype(bf16)
        x_ref[...] = weight * (x_ref[...] + mm(xh, e))
        return carry

    lax.fori_loop(0, steps, newton, 0)
    x = x_ref[...]
    xh = x.astype(bf16)
    xl = (x - xh.astype(f32)).astype(bf16)
    ident = jnp.where(eye_mask(size), f32(1.0), f32(0.0))
    e = ident - (mm(ah_ref[...], xh) + (mm(ah_ref[...], xl) + mm(al_ref[...], xh)))
    e_ref[...] = e
    error = jnp.sum(e * e)

    def full_residual():
        ident = jnp.where(eye_mask(size), f32(1.0), f32(0.0))
        e = ident - mm_full(a_ref[...], x_ref[...])
        e_ref[...] = e
        return jnp.sum(e * e)

    def restart():
        ident = jnp.where(eye_mask(size), f32(1.0), f32(0.0))
        x_ref[...] = (1.0 / upper)[:1, :1] * ident
        return full_residual()

    error = lax.cond(error < 0.2, lambda: error, restart)

    def more(state):
        return (state[1] > 1e-3) & (state[0] < 60)

    def refine(state):
        x_ref[...] = x_ref[...] + mm_full(x_ref[...], e_ref[...])
        return (state[0] + 1, full_residual())

    lax.while_loop(more, refine, (jnp.int32(0), error))
    x_ref[...] = x_ref[...] + mm(x_ref[...].astype(bf16), e_ref[...].astype(bf16))


def chain_kernel(
    own_ref, g_ref, h_ref, frow_ref, fcol_ref, qrow_ref, qcol_ref,
    mean_ref, var_ref, smooth_ref,
    m_ref, lam_ref, y_ref, prior_row_ref, prior_col_ref, own_y_ref,
    a_ref, x_ref, e_ref, ah_ref, al_ref, r_ref, pr_row_ref, pr_col_ref,
):
    steps, size = g_ref.shape[0], g_ref.shape[1]
    own = own_ref[0]
    frow, fcol = frow_ref[...], fcol_ref[...]
    sq_row, sq_col = jnp.sqrt(qrow_ref[...]), jnp.sqrt(qcol_ref[...])
    f2_row, f2_col = frow * frow, fcol * fcol
    prior_row_ref[...] = jnp.ones_like(prior_row_ref)
    prior_col_ref[...] = jnp.ones_like(prior_col_ref)

    def step(index, carry):
        @pl.when(index < steps)
        def _():
            before = jnp.maximum(index - 1, 0)
            keep = jnp.where(index > 0, f32(1.0), f32(0.0))
            ident = jnp.where(eye_mask(size), f32(1.0), f32(0.0))
            moved = jnp.where(index > 0, m_ref[before] * (fcol * frow), 0.0)
            lam = g_ref[jnp.minimum(index, steps - 1)] * (sq_col * sq_row) + (ident - moved)
            y = h_ref[jnp.minimum(index, steps - 1)] * sq_row

            @pl.when(index == 0)
            def _():
                y_ref[0] = y

            @pl.when(index > 0)
            def _():
                y_ref[index] = y + frow * vec_mat(y_ref[before], m_ref[before])
                prior_row_ref[...] = prior_row_ref[...] / (prior_row_ref[...] + f2_row)
                prior_col_ref[...] = prior_col_ref[...] / (prior_col_ref[...] + f2_col)

            @pl.when(index == own)
            def _():
                lam_ref[...] = lam
                pr_row_ref[...] = prior_row_ref[...]
                pr_col_ref[...] = prior_col_ref[...]
                own_y_ref[...] = y_ref[index]

            a_ref[...] = lam

        last = index >= steps - 1
        extra = jnp.where(last, f32(0.0), f32(1.0))

        @pl.when(index == steps)
        def _():
            a_ref[...] = lam_ref[...]
            prior_row_ref[...] = pr_row_ref[...]
            prior_col_ref[...] = pr_col_ref[...]

        row_scale = lax.rsqrt(prior_row_ref[...] + extra * f2_row)
        col_scale = lax.rsqrt(prior_col_ref[...] + extra * f2_col)
        diagonal = jnp.where(eye_mask(size), extra * f2_row, 0.0)
        a_ref[...] = (a_ref[...] + diagonal) * (col_scale * row_scale)
        inverse(a_ref, x_ref, e_ref, ah_ref, al_ref, r_ref)
        m_ref[index] = x_ref[...] * (col_scale * row_scale)
        return carry

    lax.fori_loop(0, steps + 1, step, 0)
    covariance = m_ref[steps]
    mean_ref[...] = sq_row * vec_mat(own_y_ref[...], covariance)
    diagonal = jnp.sum(jnp.where(eye_mask(size), covariance, 0.0), axis=0, keepdims=True)
    var_ref[...] = qrow_ref[...] * diagonal
    final = vec_mat(y_ref[steps - 1], m_ref[steps - 1])

    def back(count, later):
        index = steps - 2 - count
        return vec_mat(y_ref[index] + frow * later, m_ref[index])

    smooth_ref[...] = sq_row * lax.fori_loop(0, steps - 1 - own, back, final)


def chain(own, matrices, vectors, persistence, shock_var):
    steps, size = matrices.shape[0], matrices.shape[1]
    row = jax.ShapeDtypeStruct((1, size), f32)
    square = pltpu.VMEM((size, size), f32)
    half = pltpu.VMEM((size, size), bf16)
    flat = pltpu.VMEM((1, size), f32)
    tall = pltpu.VMEM((size, 1), f32)
    whole = pl.BlockSpec(memory_space=pltpu.VMEM)
    return pl.pallas_call(
        chain_kernel,
        out_shape=(row, row, row),
        in_specs=[pl.BlockSpec(memory_space=pltpu.SMEM)] + [whole] * 6,
        out_specs=(whole, whole, whole),
        scratch_shapes=[
            pltpu.VMEM((steps + 1, size, size), f32), square, pltpu.VMEM((steps, 1, size), f32),
            flat, tall, flat, square, square, square, half, half,
            pltpu.VMEM((8, 128), f32), flat, tall,
        ],
        compiler_params=pltpu.CompilerParams(vmem_limit_bytes=56 * 1024 * 1024),
    )(
        own, matrices, vectors[:, None, :], persistence[None, :], persistence[:, None],
        shock_var[None, :], shock_var[:, None],
    )


def step_information(loadings, noise_var, row_quotes, row_present):
    scaled = row_present.astype(f32) / noise_var
    weighted = (loadings.astype(f32) * scaled[:, None]).astype(bf16)
    info_matrix = lax.dot_general(
        weighted, loadings, (((0,), (0,)), ((), ())), preferred_element_type=f32
    )
    info_vector = jnp.dot(row_quotes, weighted.astype(f32), precision=highest)
    return (info_matrix, info_vector)


def body(quotes, present, loadings, noise_var, persistence, shock_var):
    parts = step_information(loadings, noise_var, quotes[0], present[0])
    parts = lax.psum(parts, "inst")
    matrices, vectors = lax.all_gather(parts, "tm")
    own = lax.axis_index("tm").astype(jnp.int32)[None]
    return chain(own, matrices, vectors, persistence, shock_var)


def solution(mesh):
    placed = (
        P(("group", "tm"), "inst"),
        P(("group", "tm"), "inst"),
        P("inst", None),
        P("inst"),
        P(),
        P(),
    )
    return jax.shard_map(
        body,
        mesh=mesh,
        in_specs=placed,
        out_specs=(P(("group", "tm"), None), P(("group", "tm"), None), P(("group", "tm"), None)),
        check_vma=False,
    )
```

```python
import functools

import jax
import jax.numpy as jnp
from jax import lax
from jax.experimental import pallas as pl
from jax.experimental.pallas import tpu as pltpu
from jax.sharding import PartitionSpec as P

f32 = jnp.float32
bf16 = jnp.bfloat16
highest = lax.Precision.HIGHEST


def mm(left, right):
    return jnp.dot(left, right, preferred_element_type=f32)


def mm_full(left, right):
    return jnp.dot(left, right, precision=highest, preferred_element_type=f32)


def eye_mask(size):
    rows = lax.broadcasted_iota(jnp.int32, (size, size), 0)
    columns = lax.broadcasted_iota(jnp.int32, (size, size), 1)
    return rows == columns


def vec_mat(vector, matrix):
    high = vector.astype(bf16).astype(f32)
    low = vector - high
    index = lax.broadcasted_iota(jnp.int32, (16, vector.shape[1]), 0)
    rows = jnp.where(index == 0, high, jnp.where(index == 1, low, 0.0)).astype(bf16)
    m_high = matrix.astype(bf16)
    m_low = (matrix - m_high.astype(f32)).astype(bf16)
    return jnp.sum(mm(rows, m_high) + mm(rows, m_low), axis=0, keepdims=True)


def inverse(a_ref, x_ref, e_ref, ah_ref, al_ref, r_ref):
    size = a_ref.shape[0]
    a = a_ref[...]
    ah = a.astype(bf16)
    ah_ref[...] = ah
    al_ref[...] = (a - ah.astype(f32)).astype(bf16)
    square = mm(ah, ah)
    fourth = jnp.full((8, 128), jnp.sum(square * square), f32)
    upper = jnp.maximum(jnp.sqrt(jnp.sqrt(fourth)) * 1.01, 1.5)
    lower = 0.98
    slope = 2.0 / (upper - lower)
    centre = (upper + lower) / (upper - lower)
    height = 1.0 / ((4.0 * centre * centre - 3.0) * centre)
    c0 = (12.0 * centre * centre - 3.0) * slope * height
    c1 = -12.0 * centre * slope * slope * height
    c2 = 4.0 * slope * slope * slope * height
    ident = jnp.where(eye_mask(size), f32(1.0), f32(0.0))
    x_ref[...] = c0[:1, :1] * ident + c1[:1, :1] * a_ref[...] + c2[:1, :1] * square
    r_ref[...] = height
    count = jnp.zeros((8, 128), f32)
    rate = height
    for _ in range(12):
        count = count + jnp.where(rate > 0.02, 1.0, 0.0)
        rate = rate * rate / (2.0 - rate * rate)
    steps = jnp.max(count).astype(jnp.int32)

    def newton(_, carry):
        rate = r_ref[...]
        r_ref[...] = rate * rate / (2.0 - rate * rate)
        weight = (2.0 / (2.0 - rate * rate))[:1, :1]
        xh = x_ref[...].astype(bf16)
        ident = jnp.where(eye_mask(size), f32(1.0), f32(0.0))
        e = (ident - mm(ah_ref[...], xh)).astype(bf16)
        x_ref[...] = weight * (x_ref[...] + mm(xh, e))
        return carry

    lax.fori_loop(0, steps, newton, 0)
    x = x_ref[...]
    xh = x.astype(bf16)
    xl = (x - xh.astype(f32)).astype(bf16)
    ident = jnp.where(eye_mask(size), f32(1.0), f32(0.0))
    e = ident - (mm(ah_ref[...], xh) + (mm(ah_ref[...], xl) + mm(al_ref[...], xh)))
    e_ref[...] = e
    error = jnp.sum(e * e)

    def full_residual():
        ident = jnp.where(eye_mask(size), f32(1.0), f32(0.0))
        e = ident - mm_full(a_ref[...], x_ref[...])
        e_ref[...] = e
        return jnp.sum(e * e)

    def restart():
        ident = jnp.where(eye_mask(size), f32(1.0), f32(0.0))
        x_ref[...] = (1.0 / upper)[:1, :1] * ident
        return full_residual()

    error = lax.cond(error < 0.2, lambda: error, restart)

    def more(state):
        return (state[1] > 1e-3) & (state[0] < 60)

    def refine(state):
        x_ref[...] = x_ref[...] + mm_full(x_ref[...], e_ref[...])
        return (state[0] + 1, full_residual())

    lax.while_loop(more, refine, (jnp.int32(0), error))
    x_ref[...] = x_ref[...] + mm(x_ref[...].astype(bf16), e_ref[...].astype(bf16))


piece = 32
MESH = pl.DeviceIdType.MESH


def pieces_of(size):
    blocks = size // 128
    return [
        (row, column, part)
        for row in range(blocks)
        for column in range(row + 1)
        for part in range(128 // piece)
    ]


def spread_kernel(insts, times, g_ref, h_ref, all_ref, pack, landed, *sems):
    rs_send, rs_recv, z_send, z_recv, x_send, x_recv, s_send, s_recv = sems
    size = g_ref.shape[0]
    t, z = lax.axis_index("tm"), lax.axis_index("inst")
    pairs = times // 2
    spot, core = t // 2, t % 2
    sibling = t + 1 - 2 * core
    z_peers = [lax.rem(z + k, insts) for k in range(insts)]
    z_from = [lax.rem(z - k + insts, insts) for k in range(insts)]
    t_peers = [lax.rem(spot + j, pairs) * 2 + core for j in range(pairs)]
    t_from = [lax.rem(spot - j + pairs, pairs) * 2 + core for j in range(pairs)]

    barrier = pltpu.get_barrier_semaphore()
    others = [{"inst": p} for p in z_peers[1:]] + [{"tm": p} for p in t_peers[1:] + [sibling]]
    for other in others:
        pl.semaphore_signal(barrier, inc=1, device_id=other, device_id_type=MESH)

    places = pieces_of(size)
    per = len(places) // insts
    tail = per * piece
    for number, (row, column, part) in enumerate(places):
        pack[number // per, pl.ds((number % per) * piece, piece), :] = g_ref[
            pl.ds(row * 128 + part * piece, piece), pl.ds(column * 128, 128)
        ]
    for chunk in range(insts):
        pack[chunk, pl.ds(tail, 8), :] = jnp.zeros((8, 128), f32)
    for row in range(size // 128):
        pack[0, pl.ds(tail + row, 1), :] = h_ref[:, pl.ds(row * 128, 128)]
    pl.semaphore_wait(barrier, len(others))

    def remote(source, target, send, recv, device):
        return pltpu.make_async_remote_copy(
            src_ref=source, dst_ref=target, send_sem=send, recv_sem=recv,
            device_id=device, device_id_type=MESH,
        )

    sent = []

    def start(copy):
        copy.start()
        sent.append(copy)

    rs = [
        remote(pack.at[z_peers[k]], landed.at[k], rs_send.at[k], rs_recv.at[k], {"inst": z_peers[k]})
        for k in range(1, insts)
    ]
    for copy in rs:
        start(copy)
    for copy in rs:
        copy.wait_recv()
    total = pack[z]
    for k in range(1, insts):
        total = total + landed[k]
    all_ref[t, z] = total

    def along_z(k, chunk, peer):
        here = all_ref.at[t, chunk]
        return remote(here, here, z_send.at[k], z_recv.at[k], {"inst": peer})

    def along_x(j, q, step, chunk, peer):
        here = all_ref.at[step, chunk]
        return remote(here, here, x_send.at[j, q], x_recv.at[j, q], {"tm": peer})

    def to_sibling(j, q, step, chunk):
        here = all_ref.at[step, chunk]
        return remote(here, here, s_send.at[j, q], s_recv.at[j, q], {"tm": sibling})

    for k in range(1, insts):
        start(along_z(k, z, z_peers[k]))
    for q in range(insts + 1):
        if q < insts:
            chunk = z_from[q]
            if q > 0:
                along_z(q, chunk, z_peers[q]).wait_recv()
            for j in range(1, pairs):
                start(along_x(j, q, t, chunk, t_peers[j]))
            start(to_sibling(0, q, t, chunk))
        if q > 0:
            chunk = z_from[q - 1]
            for j in range(1, pairs):
                along_x(j, q - 1, t_from[j], chunk, t_peers[j]).wait_recv()
                start(to_sibling(j, q - 1, t_from[j], chunk))
    for q in range(insts):
        for j in range(pairs):
            source = t_from[j] + 1 - 2 * core
            to_sibling(j, q, source, z_from[q]).wait_recv()
    for copy in sent:
        copy.wait_send()


def spread(matrix, vector, insts, times):
    size = matrix.shape[0]
    rows = len(pieces_of(size)) // insts * piece + 8
    whole = pl.BlockSpec(memory_space=pltpu.VMEM)
    dma = pltpu.SemaphoreType.DMA
    pairs = times // 2
    return pl.pallas_call(
        functools.partial(spread_kernel, insts, times),
        out_shape=jax.ShapeDtypeStruct((times, insts, rows, 128), f32),
        in_specs=[whole, whole],
        out_specs=whole,
        scratch_shapes=[
            pltpu.VMEM((insts, rows, 128), f32), pltpu.VMEM((insts, rows, 128), f32),
            dma((insts,)), dma((insts,)), dma((insts,)), dma((insts,)),
            dma((pairs, insts)), dma((pairs, insts)), dma((pairs, insts)), dma((pairs, insts)),
        ],
        compiler_params=pltpu.CompilerParams(
            collective_id=0, has_side_effects=True, vmem_limit_bytes=48 * 1024 * 1024
        ),
    )(matrix, vector[None, :])


def unpack(g_ref, index, a_ref):
    size = a_ref.shape[0]
    places = pieces_of(size)
    per = len(places) // g_ref.shape[1]
    for number, (row, column, part) in enumerate(places):
        a_ref[pl.ds(row * 128 + part * piece, piece), pl.ds(column * 128, 128)] = g_ref[
            index, number // per, pl.ds((number % per) * piece, piece), :
        ]
    for row in range(size // 128):
        for column in range(row):
            below = a_ref[pl.ds(row * 128, 128), pl.ds(column * 128, 128)]
            a_ref[pl.ds(column * 128, 128), pl.ds(row * 128, 128)] = below.T
    rows = g_ref[index, 0, pl.ds(per * piece, 8), :]
    return jnp.concatenate([rows[row : row + 1] for row in range(size // 128)], axis=1)


def chain_kernel(
    own_ref, g_ref, frow_ref, fcol_ref, qrow_ref, qcol_ref,
    mean_ref, var_ref, smooth_ref,
    m_ref, lam_ref, y_ref, prior_row_ref, prior_col_ref, own_y_ref,
    a_ref, x_ref, e_ref, ah_ref, al_ref, r_ref, pr_row_ref, pr_col_ref,
):
    steps, size = g_ref.shape[0], frow_ref.shape[1]
    own = own_ref[0]
    frow, fcol = frow_ref[...], fcol_ref[...]
    sq_row, sq_col = jnp.sqrt(qrow_ref[...]), jnp.sqrt(qcol_ref[...])
    f2_row, f2_col = frow * frow, fcol * fcol
    prior_row_ref[...] = jnp.ones_like(prior_row_ref)
    prior_col_ref[...] = jnp.ones_like(prior_col_ref)

    def step(index, carry):
        @pl.when(index < steps)
        def _():
            before = jnp.maximum(index - 1, 0)
            keep = jnp.where(index > 0, f32(1.0), f32(0.0))
            ident = jnp.where(eye_mask(size), f32(1.0), f32(0.0))
            moved = jnp.where(index > 0, m_ref[before] * (fcol * frow), 0.0)
            y = unpack(g_ref, index, a_ref) * sq_row
            lam = a_ref[...] * (sq_col * sq_row) + (ident - moved)

            @pl.when(index == 0)
            def _():
                y_ref[0] = y

            @pl.when(index > 0)
            def _():
                y_ref[index] = y + frow * vec_mat(y_ref[before], m_ref[before])
                prior_row_ref[...] = prior_row_ref[...] / (prior_row_ref[...] + f2_row)
                prior_col_ref[...] = prior_col_ref[...] / (prior_col_ref[...] + f2_col)

            @pl.when(index == own)
            def _():
                lam_ref[...] = lam
                pr_row_ref[...] = prior_row_ref[...]
                pr_col_ref[...] = prior_col_ref[...]
                own_y_ref[...] = y_ref[index]

            a_ref[...] = lam

        last = index >= steps - 1
        extra = jnp.where(last, f32(0.0), f32(1.0))

        @pl.when(index == steps)
        def _():
            a_ref[...] = lam_ref[...]
            prior_row_ref[...] = pr_row_ref[...]
            prior_col_ref[...] = pr_col_ref[...]

        row_scale = lax.rsqrt(prior_row_ref[...] + extra * f2_row)
        col_scale = lax.rsqrt(prior_col_ref[...] + extra * f2_col)
        diagonal = jnp.where(eye_mask(size), extra * f2_row, 0.0)
        a_ref[...] = (a_ref[...] + diagonal) * (col_scale * row_scale)
        inverse(a_ref, x_ref, e_ref, ah_ref, al_ref, r_ref)
        m_ref[index] = x_ref[...] * (col_scale * row_scale)
        return carry

    lax.fori_loop(0, steps + 1, step, 0)
    covariance = m_ref[steps]
    mean_ref[...] = sq_row * vec_mat(own_y_ref[...], covariance)
    diagonal = jnp.sum(jnp.where(eye_mask(size), covariance, 0.0), axis=0, keepdims=True)
    var_ref[...] = qrow_ref[...] * diagonal
    final = vec_mat(y_ref[steps - 1], m_ref[steps - 1])

    def back(count, later):
        index = steps - 2 - count
        return vec_mat(y_ref[index] + frow * later, m_ref[index])

    smooth_ref[...] = sq_row * lax.fori_loop(0, steps - 1 - own, back, final)


def chain(own, matrices, persistence, shock_var):
    steps, size = matrices.shape[0], persistence.shape[0]
    row = jax.ShapeDtypeStruct((1, size), f32)
    square = pltpu.VMEM((size, size), f32)
    half = pltpu.VMEM((size, size), bf16)
    flat = pltpu.VMEM((1, size), f32)
    tall = pltpu.VMEM((size, 1), f32)
    whole = pl.BlockSpec(memory_space=pltpu.VMEM)
    return pl.pallas_call(
        chain_kernel,
        out_shape=(row, row, row),
        in_specs=[pl.BlockSpec(memory_space=pltpu.SMEM)] + [whole] * 5,
        out_specs=(whole, whole, whole),
        scratch_shapes=[
            pltpu.VMEM((steps + 1, size, size), f32), square, pltpu.VMEM((steps, 1, size), f32),
            flat, tall, flat, square, square, square, half, half,
            pltpu.VMEM((8, 128), f32), flat, tall,
        ],
        compiler_params=pltpu.CompilerParams(vmem_limit_bytes=56 * 1024 * 1024),
    )(
        own, matrices, persistence[None, :], persistence[:, None],
        shock_var[None, :], shock_var[:, None],
    )


def step_information(loadings, noise_var, row_quotes, row_present):
    scaled = row_present.astype(f32) / noise_var
    weighted = (loadings.astype(f32) * scaled[:, None]).astype(bf16)
    info_matrix = lax.dot_general(
        weighted, loadings, (((0,), (0,)), ((), ())), preferred_element_type=f32
    )
    info_vector = jnp.dot(row_quotes, weighted.astype(f32), precision=highest)
    return (info_matrix, info_vector)


def body(quotes, present, loadings, noise_var, persistence, shock_var):
    parts = step_information(loadings, noise_var, quotes[0], present[0])
    matrices = spread(*parts, lax.axis_size("inst"), lax.axis_size("tm"))
    own = lax.axis_index("tm").astype(jnp.int32)[None]
    return chain(own, matrices, persistence, shock_var)


def solution(mesh):
    placed = (
        P(("group", "tm"), "inst"),
        P(("group", "tm"), "inst"),
        P("inst", None),
        P("inst"),
        P(),
        P(),
    )
    return jax.shard_map(
        body,
        mesh=mesh,
        in_specs=placed,
        out_specs=(P(("group", "tm"), None), P(("group", "tm"), None), P(("group", "tm"), None)),
        check_vma=False,
    )
```

```python
import functools

import jax
import jax.numpy as jnp
from jax import lax
from jax.experimental import pallas as pl
from jax.experimental.pallas import tpu as pltpu
from jax.sharding import PartitionSpec as P

f32 = jnp.float32
bf16 = jnp.bfloat16
highest = lax.Precision.HIGHEST


def mm(left, right):
    return jnp.dot(left, right, preferred_element_type=f32)


def mm_full(left, right):
    return jnp.dot(left, right, precision=highest, preferred_element_type=f32)


def eye_mask(size):
    rows = lax.broadcasted_iota(jnp.int32, (size, size), 0)
    columns = lax.broadcasted_iota(jnp.int32, (size, size), 1)
    return rows == columns


def vec_mat(vector, matrix):
    high = vector.astype(bf16).astype(f32)
    low = vector - high
    index = lax.broadcasted_iota(jnp.int32, (16, vector.shape[1]), 0)
    rows = jnp.where(index == 0, high, jnp.where(index == 1, low, 0.0)).astype(bf16)
    m_high = matrix.astype(bf16)
    m_low = (matrix - m_high.astype(f32)).astype(bf16)
    return jnp.sum(mm(rows, m_high) + mm(rows, m_low), axis=0, keepdims=True)


def inverse(a_ref, x_ref, e_ref, ah_ref, r_ref, ident_ref):
    a = a_ref[...]
    ah = a.astype(bf16)
    ah_ref[...] = ah
    square = mm(ah, ah)
    fourth = jnp.full((8, 128), jnp.sum(square * square), f32)
    upper = jnp.maximum(jnp.sqrt(jnp.sqrt(fourth)) * 1.01, 1.5)
    lower = 0.98
    slope = 2.0 / (upper - lower)
    centre = (upper + lower) / (upper - lower)
    height = 1.0 / ((4.0 * centre * centre - 3.0) * centre)
    c0 = (12.0 * centre * centre - 3.0) * slope * height
    c1 = -12.0 * centre * slope * slope * height
    c2 = 4.0 * slope * slope * slope * height
    x_ref[...] = c0[:1, :1] * ident_ref[...] + c1[:1, :1] * a_ref[...] + c2[:1, :1] * square
    r_ref[...] = height
    count = jnp.zeros((8, 128), f32)
    rate = height
    for _ in range(12):
        count = count + jnp.where(rate > 0.02, 1.0, 0.0)
        rate = rate * rate / (2.0 - rate * rate)
    steps = jnp.max(count).astype(jnp.int32)

    def newton(_, carry):
        rate = r_ref[...]
        r_ref[...] = rate * rate / (2.0 - rate * rate)
        weight = (2.0 / (2.0 - rate * rate))[:1, :1]
        xh = x_ref[...].astype(bf16)
        e = (ident_ref[...] - mm(ah_ref[...], xh)).astype(bf16)
        x_ref[...] = weight * (x_ref[...] + mm(xh, e))
        return carry

    lax.fori_loop(0, steps, newton, 0)
    x = x_ref[...]
    xh = x.astype(bf16)
    xl = (x - xh.astype(f32)).astype(bf16)
    a = a_ref[...]
    al = (a - a.astype(bf16).astype(f32)).astype(bf16)
    e = ident_ref[...] - (mm(ah_ref[...], xh) + (mm(ah_ref[...], xl) + mm(al, xh)))
    eh = e.astype(bf16)
    twice = mm(eh, eh)
    e_ref[...] = e + twice
    small = jnp.sum(twice * twice) < 1e-4

    @pl.when(jnp.logical_not(small))
    def _():
        x_ref[...] = (1.0 / upper)[:1, :1] * ident_ref[...]

        def residual():
            e = ident_ref[...] - mm_full(a_ref[...], x_ref[...])
            e_ref[...] = e
            return jnp.sum(e * e)

        def more(state):
            return (state[1] > 1e-3) & (state[0] < 60)

        def refine(state):
            x_ref[...] = x_ref[...] + mm_full(x_ref[...], e_ref[...])
            return (state[0] + 1, residual())

        lax.while_loop(more, refine, (jnp.int32(0), residual()))

    x_ref[...] = x_ref[...] + mm(x_ref[...].astype(bf16), e_ref[...].astype(bf16))


piece = 32
MESH = pl.DeviceIdType.MESH


def pieces_of(size):
    blocks = size // 128
    return [
        (row, column, part)
        for row in range(blocks)
        for column in range(row + 1)
        for part in range(128 // piece)
    ]


def spread_kernel(insts, times, g_ref, h_ref, all_ref, pack, landed, *sems):
    rs_send, rs_recv, z_send, z_recv, x_send, x_recv, s_send, s_recv = sems
    size = g_ref.shape[0]
    t, z = lax.axis_index("tm"), lax.axis_index("inst")
    pairs = times // 2
    spot, core = t // 2, t % 2
    sibling = t + 1 - 2 * core
    z_peers = [lax.rem(z + k, insts) for k in range(insts)]
    z_from = [lax.rem(z - k + insts, insts) for k in range(insts)]
    t_peers = [lax.rem(spot + j, pairs) * 2 + core for j in range(pairs)]
    t_from = [lax.rem(spot - j + pairs, pairs) * 2 + core for j in range(pairs)]

    barrier = pltpu.get_barrier_semaphore()
    others = [{"inst": p} for p in z_peers[1:]] + [{"tm": p} for p in t_peers[1:] + [sibling]]
    for other in others:
        pl.semaphore_signal(barrier, inc=1, device_id=other, device_id_type=MESH)

    places = pieces_of(size)
    per = len(places) // insts
    tail = per * piece
    for number, (row, column, part) in enumerate(places):
        pack[number // per, pl.ds((number % per) * piece, piece), :] = g_ref[
            pl.ds(row * 128 + part * piece, piece), pl.ds(column * 128, 128)
        ]
    for chunk in range(insts):
        pack[chunk, pl.ds(tail, 8), :] = jnp.zeros((8, 128), f32)
    for row in range(size // 128):
        pack[0, pl.ds(tail + row, 1), :] = h_ref[:, pl.ds(row * 128, 128)]
    pl.semaphore_wait(barrier, len(others))

    def remote(source, target, send, recv, device):
        return pltpu.make_async_remote_copy(
            src_ref=source, dst_ref=target, send_sem=send, recv_sem=recv,
            device_id=device, device_id_type=MESH,
        )

    sent = []

    def start(copy):
        copy.start()
        sent.append(copy)

    rs = [
        remote(pack.at[z_peers[k]], landed.at[k], rs_send.at[k], rs_recv.at[k], {"inst": z_peers[k]})
        for k in range(1, insts)
    ]
    for copy in rs:
        start(copy)
    for copy in rs:
        copy.wait_recv()
    total = pack[z]
    for k in range(1, insts):
        total = total + landed[k]
    all_ref[t, z] = total

    def along_z(k, chunk, peer):
        here = all_ref.at[t, chunk]
        return remote(here, here, z_send.at[k], z_recv.at[k], {"inst": peer})

    def along_x(j, q, step, chunk, peer):
        here = all_ref.at[step, chunk]
        return remote(here, here, x_send.at[j, q], x_recv.at[j, q], {"tm": peer})

    def to_sibling(j, q, step, chunk):
        here = all_ref.at[step, chunk]
        return remote(here, here, s_send.at[j, q], s_recv.at[j, q], {"tm": sibling})

    for k in range(1, insts):
        start(along_z(k, z, z_peers[k]))
    for q in range(insts + 1):
        if q < insts:
            chunk = z_from[q]
            if q > 0:
                along_z(q, chunk, z_peers[q]).wait_recv()
            for j in range(1, pairs):
                start(along_x(j, q, t, chunk, t_peers[j]))
            start(to_sibling(0, q, t, chunk))
        if q > 0:
            chunk = z_from[q - 1]
            for j in range(1, pairs):
                along_x(j, q - 1, t_from[j], chunk, t_peers[j]).wait_recv()
                start(to_sibling(j, q - 1, t_from[j], chunk))
    for q in range(insts):
        for j in range(pairs):
            source = t_from[j] + 1 - 2 * core
            to_sibling(j, q, source, z_from[q]).wait_recv()
    for copy in sent:
        copy.wait_send()


def spread(matrix, vector, insts, times):
    size = matrix.shape[0]
    rows = len(pieces_of(size)) // insts * piece + 8
    whole = pl.BlockSpec(memory_space=pltpu.VMEM)
    dma = pltpu.SemaphoreType.DMA
    pairs = times // 2
    return pl.pallas_call(
        functools.partial(spread_kernel, insts, times),
        out_shape=jax.ShapeDtypeStruct((times, insts, rows, 128), f32),
        in_specs=[whole, whole],
        out_specs=whole,
        scratch_shapes=[
            pltpu.VMEM((insts, rows, 128), f32), pltpu.VMEM((insts, rows, 128), f32),
            dma((insts,)), dma((insts,)), dma((insts,)), dma((insts,)),
            dma((pairs, insts)), dma((pairs, insts)), dma((pairs, insts)), dma((pairs, insts)),
        ],
        compiler_params=pltpu.CompilerParams(
            collective_id=0, has_side_effects=True, vmem_limit_bytes=48 * 1024 * 1024
        ),
    )(matrix, vector[None, :])


def unpack(g_ref, index, a_ref):
    size = a_ref.shape[0]
    places = pieces_of(size)
    per = len(places) // g_ref.shape[1]
    for number, (row, column, part) in enumerate(places):
        a_ref[pl.ds(row * 128 + part * piece, piece), pl.ds(column * 128, 128)] = g_ref[
            index, number // per, pl.ds((number % per) * piece, piece), :
        ]
    for row in range(size // 128):
        for column in range(row):
            below = a_ref[pl.ds(row * 128, 128), pl.ds(column * 128, 128)]
            a_ref[pl.ds(column * 128, 128), pl.ds(row * 128, 128)] = below.T
    rows = g_ref[index, 0, pl.ds(per * piece, 8), :]
    return jnp.concatenate([rows[row : row + 1] for row in range(size // 128)], axis=1)


def chain_kernel(
    own_ref, g_ref, frow_ref, fcol_ref, qrow_ref, qcol_ref,
    mean_ref, var_ref, smooth_ref,
    m_ref, lam_ref, y_ref, prior_row_ref, prior_col_ref, own_y_ref,
    a_ref, x_ref, e_ref, ah_ref, ident_ref, r_ref, pr_row_ref, pr_col_ref,
):
    steps, size = g_ref.shape[0], frow_ref.shape[1]
    own = own_ref[0]
    frow, fcol = frow_ref[...], fcol_ref[...]
    sq_row, sq_col = jnp.sqrt(qrow_ref[...]), jnp.sqrt(qcol_ref[...])
    f2_row, f2_col = frow * frow, fcol * fcol
    ident_ref[...] = jnp.where(eye_mask(size), f32(1.0), f32(0.0))
    prior_row_ref[...] = jnp.ones_like(prior_row_ref)
    prior_col_ref[...] = jnp.ones_like(prior_col_ref)

    def step(index, carry):
        @pl.when(index < steps)
        def _():
            before = jnp.maximum(index - 1, 0)
            moved = jnp.where(index > 0, m_ref[before] * (fcol * frow), 0.0)
            y = unpack(g_ref, index, a_ref) * sq_row
            lam = a_ref[...] * (sq_col * sq_row) + (ident_ref[...] - moved)

            @pl.when(index == 0)
            def _():
                y_ref[0] = y

            @pl.when(index > 0)
            def _():
                y_ref[index] = y + frow * vec_mat(y_ref[before], m_ref[before])
                prior_row_ref[...] = prior_row_ref[...] / (prior_row_ref[...] + f2_row)
                prior_col_ref[...] = prior_col_ref[...] / (prior_col_ref[...] + f2_col)

            @pl.when(index == own)
            def _():
                lam_ref[...] = lam
                pr_row_ref[...] = prior_row_ref[...]
                pr_col_ref[...] = prior_col_ref[...]
                own_y_ref[...] = y_ref[index]

            a_ref[...] = lam

        last = index >= steps - 1
        extra = jnp.where(last, f32(0.0), f32(1.0))

        @pl.when(index == steps)
        def _():
            a_ref[...] = lam_ref[...]
            prior_row_ref[...] = pr_row_ref[...]
            prior_col_ref[...] = pr_col_ref[...]

        row_scale = lax.rsqrt(prior_row_ref[...] + extra * f2_row)
        col_scale = lax.rsqrt(prior_col_ref[...] + extra * f2_col)
        diagonal = ident_ref[...] * (extra * f2_row)
        a_ref[...] = (a_ref[...] + diagonal) * (col_scale * row_scale)
        inverse(a_ref, x_ref, e_ref, ah_ref, r_ref, ident_ref)
        m_ref[index] = x_ref[...] * (col_scale * row_scale)
        return carry

    lax.fori_loop(0, steps + 1, step, 0)
    covariance = m_ref[steps]
    mean_ref[...] = sq_row * vec_mat(own_y_ref[...], covariance)
    diagonal = jnp.sum(ident_ref[...] * covariance, axis=0, keepdims=True)
    var_ref[...] = qrow_ref[...] * diagonal
    final = vec_mat(y_ref[steps - 1], m_ref[steps - 1])

    def back(count, later):
        index = steps - 2 - count
        return vec_mat(y_ref[index] + frow * later, m_ref[index])

    smooth_ref[...] = sq_row * lax.fori_loop(0, steps - 1 - own, back, final)


def chain(own, matrices, persistence, shock_var):
    steps, size = matrices.shape[0], persistence.shape[0]
    row = jax.ShapeDtypeStruct((1, size), f32)
    square = pltpu.VMEM((size, size), f32)
    half = pltpu.VMEM((size, size), bf16)
    flat = pltpu.VMEM((1, size), f32)
    tall = pltpu.VMEM((size, 1), f32)
    whole = pl.BlockSpec(memory_space=pltpu.VMEM)
    return pl.pallas_call(
        chain_kernel,
        out_shape=(row, row, row),
        in_specs=[pl.BlockSpec(memory_space=pltpu.SMEM)] + [whole] * 5,
        out_specs=(whole, whole, whole),
        scratch_shapes=[
            pltpu.VMEM((steps + 1, size, size), f32), square, pltpu.VMEM((steps, 1, size), f32),
            flat, tall, flat, square, square, square, half, square,
            pltpu.VMEM((8, 128), f32), flat, tall,
        ],
        compiler_params=pltpu.CompilerParams(vmem_limit_bytes=56 * 1024 * 1024),
    )(
        own, matrices, persistence[None, :], persistence[:, None],
        shock_var[None, :], shock_var[:, None],
    )


def step_information(loadings, noise_var, row_quotes, row_present):
    scaled = row_present.astype(f32) / noise_var
    weighted = (loadings.astype(f32) * scaled[:, None]).astype(bf16)
    info_matrix = lax.dot_general(
        weighted, loadings, (((0,), (0,)), ((), ())), preferred_element_type=f32
    )
    info_vector = jnp.dot(row_quotes, weighted.astype(f32), precision=highest)
    return (info_matrix, info_vector)


def body(quotes, present, loadings, noise_var, persistence, shock_var):
    parts = step_information(loadings, noise_var, quotes[0], present[0])
    matrices = spread(*parts, lax.axis_size("inst"), lax.axis_size("tm"))
    own = lax.axis_index("tm").astype(jnp.int32)[None]
    return chain(own, matrices, persistence, shock_var)


def solution(mesh):
    placed = (
        P(("group", "tm"), "inst"),
        P(("group", "tm"), "inst"),
        P("inst", None),
        P("inst"),
        P(),
        P(),
    )
    return jax.shard_map(
        body,
        mesh=mesh,
        in_specs=placed,
        out_specs=(P(("group", "tm"), None), P(("group", "tm"), None), P(("group", "tm"), None)),
        check_vma=False,
    )
```

```python
import functools

import jax
import jax.numpy as jnp
from jax import lax
from jax.experimental import pallas as pl
from jax.experimental.pallas import tpu as pltpu
from jax.sharding import PartitionSpec as P

f32 = jnp.float32
bf16 = jnp.bfloat16
highest = lax.Precision.HIGHEST


def mm(left, right):
    return jnp.dot(left, right, preferred_element_type=f32)


def mm_full(left, right):
    return jnp.dot(left, right, precision=highest, preferred_element_type=f32)


def eye_mask(size):
    rows = lax.broadcasted_iota(jnp.int32, (size, size), 0)
    columns = lax.broadcasted_iota(jnp.int32, (size, size), 1)
    return rows == columns


def vec_mat(vector, matrix):
    high = vector.astype(bf16).astype(f32)
    low = vector - high
    index = lax.broadcasted_iota(jnp.int32, (16, vector.shape[1]), 0)
    rows = jnp.where(index == 0, high, jnp.where(index == 1, low, 0.0)).astype(bf16)
    m_high = matrix.astype(bf16)
    m_low = (matrix - m_high.astype(f32)).astype(bf16)
    return jnp.sum(mm(rows, m_high) + mm(rows, m_low), axis=0, keepdims=True)


def inverse(a_ref, x_ref, e_ref, ah_ref, r_ref, ident_ref):
    a = a_ref[...]
    ah = a.astype(bf16)
    ah_ref[...] = ah
    square = mm(ah, ah)
    fourth = jnp.full((8, 128), jnp.sum(square * square), f32)
    upper = jnp.maximum(jnp.sqrt(jnp.sqrt(fourth)) * 1.01, 1.5)
    lower = 0.98
    slope = 2.0 / (upper - lower)
    centre = (upper + lower) / (upper - lower)
    height = 1.0 / ((4.0 * centre * centre - 3.0) * centre)
    c0 = (12.0 * centre * centre - 3.0) * slope * height
    c1 = -12.0 * centre * slope * slope * height
    c2 = 4.0 * slope * slope * slope * height
    x_ref[...] = c0[:1, :1] * ident_ref[...] + c1[:1, :1] * a_ref[...] + c2[:1, :1] * square
    r_ref[...] = height
    count = jnp.zeros((8, 128), f32)
    rate = height
    for _ in range(12):
        count = count + jnp.where(rate > 0.02, 1.0, 0.0)
        rate = rate * rate / (2.0 - rate * rate)
    steps = jnp.max(count).astype(jnp.int32)

    def newton(_, carry):
        rate = r_ref[...]
        r_ref[...] = rate * rate / (2.0 - rate * rate)
        weight = (2.0 / (2.0 - rate * rate))[:1, :1]
        xh = x_ref[...].astype(bf16)
        e = (ident_ref[...] - mm(ah_ref[...], xh)).astype(bf16)
        x_ref[...] = weight * (x_ref[...] + mm(xh, e))
        return carry

    lax.fori_loop(0, steps, newton, 0)
    x = x_ref[...]
    xh = x.astype(bf16)
    xl = (x - xh.astype(f32)).astype(bf16)
    a = a_ref[...]
    al = (a - a.astype(bf16).astype(f32)).astype(bf16)
    e = ident_ref[...] - (mm(ah_ref[...], xh) + (mm(ah_ref[...], xl) + mm(al, xh)))
    eh = e.astype(bf16)
    twice = mm(eh, eh)
    e_ref[...] = e + twice
    small = jnp.sum(twice * twice) < 1e-4

    @pl.when(jnp.logical_not(small))
    def _():
        x_ref[...] = (1.0 / upper)[:1, :1] * ident_ref[...]

        def residual():
            e = ident_ref[...] - mm_full(a_ref[...], x_ref[...])
            e_ref[...] = e
            return jnp.sum(e * e)

        def more(state):
            return (state[1] > 1e-3) & (state[0] < 60)

        def refine(state):
            x_ref[...] = x_ref[...] + mm_full(x_ref[...], e_ref[...])
            return (state[0] + 1, residual())

        lax.while_loop(more, refine, (jnp.int32(0), residual()))

    x_ref[...] = x_ref[...] + mm(x_ref[...].astype(bf16), e_ref[...].astype(bf16))


piece = 32
MESH = pl.DeviceIdType.MESH


def pieces_of(size):
    blocks = size // 128
    return [
        (row, column, part)
        for row in range(blocks)
        for column in range(row + 1)
        for part in range(128 // piece)
    ]


def spread_kernel(insts, times, g_ref, h_ref, all_ref, pack, landed, *sems):
    rs_send, rs_recv, z_send, z_recv, x_send, x_recv, s_send, s_recv = sems
    size = g_ref.shape[0]
    t, z = lax.axis_index("tm"), lax.axis_index("inst")
    pairs = times // 2
    spot, core = t // 2, t % 2
    sibling = t + 1 - 2 * core
    z_peers = [lax.rem(z + k, insts) for k in range(insts)]
    z_from = [lax.rem(z - k + insts, insts) for k in range(insts)]
    t_peers = [lax.rem(spot + j, pairs) * 2 + core for j in range(pairs)]
    t_from = [lax.rem(spot - j + pairs, pairs) * 2 + core for j in range(pairs)]

    barrier = pltpu.get_barrier_semaphore()
    others = [{"inst": p} for p in z_peers[1:]] + [{"tm": p} for p in t_peers[1:] + [sibling]]
    for other in others:
        pl.semaphore_signal(barrier, inc=1, device_id=other, device_id_type=MESH)

    places = pieces_of(size)
    per = len(places) // insts
    tail = per * piece
    for number, (row, column, part) in enumerate(places):
        pack[number // per, pl.ds((number % per) * piece, piece), :] = g_ref[
            pl.ds(row * 128 + part * piece, piece), pl.ds(column * 128, 128)
        ]
    for chunk in range(insts):
        pack[chunk, pl.ds(tail, 8), :] = jnp.zeros((8, 128), f32)
    for row in range(size // 128):
        pack[0, pl.ds(tail + row, 1), :] = h_ref[:, pl.ds(row * 128, 128)]
    pl.semaphore_wait(barrier, len(others))

    def remote(source, target, send, recv, device):
        return pltpu.make_async_remote_copy(
            src_ref=source, dst_ref=target, send_sem=send, recv_sem=recv,
            device_id=device, device_id_type=MESH,
        )

    sent = []

    def start(copy):
        copy.start()
        sent.append(copy)

    rs = [
        remote(pack.at[z_peers[k]], landed.at[k], rs_send.at[k], rs_recv.at[k], {"inst": z_peers[k]})
        for k in range(1, insts)
    ]
    for copy in rs:
        start(copy)
    for copy in rs:
        copy.wait_recv()
    total = pack[z]
    for k in range(1, insts):
        total = total + landed[k]
    all_ref[t, z] = total

    def along_z(k, chunk, peer):
        here = all_ref.at[t, chunk]
        return remote(here, here, z_send.at[k], z_recv.at[k], {"inst": peer})

    def along_x(j, q, step, chunk, peer):
        here = all_ref.at[step, chunk]
        return remote(here, here, x_send.at[j, q], x_recv.at[j, q], {"tm": peer})

    def to_sibling(j, q, step, chunk):
        here = all_ref.at[step, chunk]
        return remote(here, here, s_send.at[j, q], s_recv.at[j, q], {"tm": sibling})

    for k in range(1, insts):
        start(along_z(k, z, z_peers[k]))
    for q in range(insts + 1):
        if q < insts:
            chunk = z_from[q]
            if q > 0:
                along_z(q, chunk, z_peers[q]).wait_recv()
            for j in range(1, pairs):
                start(along_x(j, q, t, chunk, t_peers[j]))
            start(to_sibling(0, q, t, chunk))
        if q > 0:
            chunk = z_from[q - 1]
            for j in range(1, pairs):
                along_x(j, q - 1, t_from[j], chunk, t_peers[j]).wait_recv()
                start(to_sibling(j, q - 1, t_from[j], chunk))
    for q in range(insts):
        for j in range(pairs):
            source = t_from[j] + 1 - 2 * core
            to_sibling(j, q, source, z_from[q]).wait_recv()
    for copy in sent:
        copy.wait_send()


def spread(matrix, vector, insts, times):
    size = matrix.shape[0]
    rows = len(pieces_of(size)) // insts * piece + 8
    whole = pl.BlockSpec(memory_space=pltpu.VMEM)
    dma = pltpu.SemaphoreType.DMA
    pairs = times // 2
    return pl.pallas_call(
        functools.partial(spread_kernel, insts, times),
        out_shape=jax.ShapeDtypeStruct((times, insts, rows, 128), f32),
        in_specs=[whole, whole],
        out_specs=whole,
        scratch_shapes=[
            pltpu.VMEM((insts, rows, 128), f32), pltpu.VMEM((insts, rows, 128), f32),
            dma((insts,)), dma((insts,)), dma((insts,)), dma((insts,)),
            dma((pairs, insts)), dma((pairs, insts)), dma((pairs, insts)), dma((pairs, insts)),
        ],
        compiler_params=pltpu.CompilerParams(
            collective_id=0, has_side_effects=True, vmem_limit_bytes=48 * 1024 * 1024
        ),
    )(matrix, vector)


def unpack(g_ref, index, a_ref):
    size = a_ref.shape[0]
    places = pieces_of(size)
    per = len(places) // g_ref.shape[1]
    for number, (row, column, part) in enumerate(places):
        a_ref[pl.ds(row * 128 + part * piece, piece), pl.ds(column * 128, 128)] = g_ref[
            index, number // per, pl.ds((number % per) * piece, piece), :
        ]
    for row in range(size // 128):
        for column in range(row):
            below = a_ref[pl.ds(row * 128, 128), pl.ds(column * 128, 128)]
            a_ref[pl.ds(column * 128, 128), pl.ds(row * 128, 128)] = below.T
    rows = g_ref[index, 0, pl.ds(per * piece, 8), :]
    return jnp.concatenate([rows[row : row + 1] for row in range(size // 128)], axis=1)


def chain_kernel(
    own_ref, g_ref, frow_ref, qrow_ref,
    mean_ref, var_ref, smooth_ref,
    m_ref, lam_ref, y_ref, prior_row_ref, prior_col_ref, own_y_ref,
    a_ref, x_ref, e_ref, ah_ref, ident_ref, r_ref, pr_row_ref, pr_col_ref,
):
    steps, size = g_ref.shape[0], frow_ref.shape[1]
    own = own_ref[0]
    ident_ref[...] = jnp.where(eye_mask(size), f32(1.0), f32(0.0))
    frow = frow_ref[...]
    fcol = jnp.sum(ident_ref[...] * frow, axis=1, keepdims=True)
    sq_row = jnp.sqrt(qrow_ref[...])
    sq_col = jnp.sum(ident_ref[...] * sq_row, axis=1, keepdims=True)
    f2_row, f2_col = frow * frow, fcol * fcol
    prior_row_ref[...] = jnp.ones_like(prior_row_ref)
    prior_col_ref[...] = jnp.ones_like(prior_col_ref)

    def step(index, carry):
        @pl.when(index < steps)
        def _():
            before = jnp.maximum(index - 1, 0)
            moved = jnp.where(index > 0, m_ref[before] * (fcol * frow), 0.0)
            y = unpack(g_ref, index, a_ref) * sq_row
            lam = a_ref[...] * (sq_col * sq_row) + (ident_ref[...] - moved)

            @pl.when(index == 0)
            def _():
                y_ref[0] = y

            @pl.when(index > 0)
            def _():
                y_ref[index] = y + frow * vec_mat(y_ref[before], m_ref[before])
                prior_row_ref[...] = prior_row_ref[...] / (prior_row_ref[...] + f2_row)
                prior_col_ref[...] = prior_col_ref[...] / (prior_col_ref[...] + f2_col)

            @pl.when(index == own)
            def _():
                lam_ref[...] = lam
                pr_row_ref[...] = prior_row_ref[...]
                pr_col_ref[...] = prior_col_ref[...]
                own_y_ref[...] = y_ref[index]

            a_ref[...] = lam

        last = index >= steps - 1
        extra = jnp.where(last, f32(0.0), f32(1.0))

        @pl.when(index == steps)
        def _():
            a_ref[...] = lam_ref[...]
            prior_row_ref[...] = pr_row_ref[...]
            prior_col_ref[...] = pr_col_ref[...]

        row_scale = lax.rsqrt(prior_row_ref[...] + extra * f2_row)
        col_scale = lax.rsqrt(prior_col_ref[...] + extra * f2_col)
        diagonal = ident_ref[...] * (extra * f2_row)
        a_ref[...] = (a_ref[...] + diagonal) * (col_scale * row_scale)
        inverse(a_ref, x_ref, e_ref, ah_ref, r_ref, ident_ref)
        m_ref[index] = x_ref[...] * (col_scale * row_scale)
        return carry

    lax.fori_loop(0, steps + 1, step, 0)
    covariance = m_ref[steps]
    mean_ref[...] = sq_row * vec_mat(own_y_ref[...], covariance)
    diagonal = jnp.sum(ident_ref[...] * covariance, axis=0, keepdims=True)
    var_ref[...] = qrow_ref[...] * diagonal
    final = vec_mat(y_ref[steps - 1], m_ref[steps - 1])

    def back(count, later):
        index = steps - 2 - count
        return vec_mat(y_ref[index] + frow * later, m_ref[index])

    smooth_ref[...] = sq_row * lax.fori_loop(0, steps - 1 - own, back, final)


def chain(own, matrices, persistence, shock_var):
    steps, size = matrices.shape[0], persistence.shape[0]
    row = jax.ShapeDtypeStruct((1, size), f32)
    square = pltpu.VMEM((size, size), f32)
    half = pltpu.VMEM((size, size), bf16)
    flat = pltpu.VMEM((1, size), f32)
    tall = pltpu.VMEM((size, 1), f32)
    whole = pl.BlockSpec(memory_space=pltpu.VMEM)
    return pl.pallas_call(
        chain_kernel,
        out_shape=(row, row, row),
        in_specs=[pl.BlockSpec(memory_space=pltpu.SMEM)] + [whole] * 3,
        out_specs=(whole, whole, whole),
        scratch_shapes=[
            pltpu.VMEM((steps + 1, size, size), f32), square, pltpu.VMEM((steps, 1, size), f32),
            flat, tall, flat, square, square, square, half, square,
            pltpu.VMEM((8, 128), f32), flat, tall,
        ],
        compiler_params=pltpu.CompilerParams(vmem_limit_bytes=56 * 1024 * 1024),
    )(
        own, matrices, persistence[None, :], shock_var[None, :],
    )


def information_kernel(quotes_ref, present_ref, noise_ref, loadings_ref, matrix_ref, vector_ref):
    @pl.when(pl.program_id(0) == 0)
    def _():
        matrix_ref[...] = jnp.zeros_like(matrix_ref)
        vector_ref[...] = jnp.zeros_like(vector_ref)

    loadings = loadings_ref[...]
    scaled = present_ref[...].astype(f32) / noise_ref[...]
    weighted = (loadings.T.astype(f32) * scaled).astype(bf16)
    matrix_ref[...] += mm(weighted, loadings)
    quotes = quotes_ref[...]
    high = quotes.astype(bf16).astype(f32)
    rest = quotes - high
    middle = rest.astype(bf16).astype(f32)
    index = lax.broadcasted_iota(jnp.int32, (16, quotes.shape[1]), 0)
    rows = jnp.where(index == 0, high, jnp.where(index == 1, middle, 0.0))
    rows = jnp.where(index == 2, rest - middle, rows).astype(bf16)
    sums = lax.dot_general(rows, weighted, (((1,), (1,)), ((), ())), preferred_element_type=f32)
    vector_ref[...] += jnp.sum(sums, axis=0, keepdims=True)


def step_information(loadings, noise_var, quotes, present):
    insts, size = loadings.shape
    chunk = 1024 if insts % 1024 == 0 else 512
    flat = pl.BlockSpec((1, chunk), lambda i: (0, i))
    return pl.pallas_call(
        information_kernel,
        grid=(insts // chunk,),
        out_shape=(
            jax.ShapeDtypeStruct((size, size), f32), jax.ShapeDtypeStruct((1, size), f32),
        ),
        in_specs=[flat, flat, flat, pl.BlockSpec((chunk, size), lambda i: (i, 0))],
        out_specs=(
            pl.BlockSpec((size, size), lambda i: (0, 0)), pl.BlockSpec((1, size), lambda i: (0, 0)),
        ),
        compiler_params=pltpu.CompilerParams(vmem_limit_bytes=32 * 1024 * 1024),
    )(quotes, present, noise_var[None, :], loadings)


def body(quotes, present, loadings, noise_var, persistence, shock_var):
    parts = step_information(loadings, noise_var, quotes, present)
    matrices = spread(*parts, lax.axis_size("inst"), lax.axis_size("tm"))
    own = lax.axis_index("tm").astype(jnp.int32)[None]
    return chain(own, matrices, persistence, shock_var)


def solution(mesh):
    placed = (
        P(("group", "tm"), "inst"),
        P(("group", "tm"), "inst"),
        P("inst", None),
        P("inst"),
        P(),
        P(),
    )
    return jax.shard_map(
        body,
        mesh=mesh,
        in_specs=placed,
        out_specs=(P(("group", "tm"), None), P(("group", "tm"), None), P(("group", "tm"), None)),
        check_vma=False,
    )
```

```python
import functools

import jax
import jax.numpy as jnp
from jax import lax
from jax.experimental import pallas as pl
from jax.experimental.pallas import tpu as pltpu
from jax.sharding import PartitionSpec as P

f32 = jnp.float32
bf16 = jnp.bfloat16
highest = lax.Precision.HIGHEST


def mm(left, right):
    return jnp.dot(left, right, preferred_element_type=f32)


def mm_full(left, right):
    return jnp.dot(left, right, precision=highest, preferred_element_type=f32)


def eye_mask(size):
    rows = lax.broadcasted_iota(jnp.int32, (size, size), 0)
    columns = lax.broadcasted_iota(jnp.int32, (size, size), 1)
    return rows == columns


def vec_mat(vector, matrix):
    high = vector.astype(bf16).astype(f32)
    low = vector - high
    index = lax.broadcasted_iota(jnp.int32, (16, vector.shape[1]), 0)
    rows = jnp.where(index == 0, high, jnp.where(index == 1, low, 0.0)).astype(bf16)
    m_high = matrix.astype(bf16)
    m_low = (matrix - m_high.astype(f32)).astype(bf16)
    return jnp.sum(mm(rows, m_high) + mm(rows, m_low), axis=0, keepdims=True)


def inverse(a_ref, x_ref, e_ref, ah_ref, r_ref, ident_ref):
    a = a_ref[...]
    ah = a.astype(bf16)
    ah_ref[...] = ah
    square = mm(ah, ah)
    fourth = jnp.full((8, 128), jnp.sum(square * square), f32)
    upper = jnp.maximum(jnp.sqrt(jnp.sqrt(fourth)) * 1.01, 1.5)
    lower = 0.98
    slope = 2.0 / (upper - lower)
    centre = (upper + lower) / (upper - lower)
    height = 1.0 / ((4.0 * centre * centre - 3.0) * centre)
    c0 = (12.0 * centre * centre - 3.0) * slope * height
    c1 = -12.0 * centre * slope * slope * height
    c2 = 4.0 * slope * slope * slope * height
    x_ref[...] = c0[:1, :1] * ident_ref[...] + c1[:1, :1] * a_ref[...] + c2[:1, :1] * square
    r_ref[...] = height
    count = jnp.zeros((8, 128), f32)
    rate = height
    for _ in range(12):
        count = count + jnp.where(rate > 0.02, 1.0, 0.0)
        rate = rate * rate / (2.0 - rate * rate)
    steps = jnp.max(count).astype(jnp.int32)

    def newton(_, carry):
        rate = r_ref[...]
        r_ref[...] = rate * rate / (2.0 - rate * rate)
        weight = (2.0 / (2.0 - rate * rate))[:1, :1]
        xh = x_ref[...].astype(bf16)
        e = (ident_ref[...] - mm(ah_ref[...], xh)).astype(bf16)
        x_ref[...] = weight * (x_ref[...] + mm(xh, e))
        return carry

    lax.fori_loop(0, steps, newton, 0)
    x = x_ref[...]
    xh = x.astype(bf16)
    xl = (x - xh.astype(f32)).astype(bf16)
    a = a_ref[...]
    al = (a - a.astype(bf16).astype(f32)).astype(bf16)
    e = ident_ref[...] - (mm(ah_ref[...], xh) + (mm(ah_ref[...], xl) + mm(al, xh)))
    eh = e.astype(bf16)
    twice = mm(eh, eh)
    e_ref[...] = e + twice
    small = jnp.sum(twice * twice) < 1e-4

    @pl.when(jnp.logical_not(small))
    def _():
        x_ref[...] = (1.0 / upper)[:1, :1] * ident_ref[...]

        def residual():
            e = ident_ref[...] - mm_full(a_ref[...], x_ref[...])
            e_ref[...] = e
            return jnp.sum(e * e)

        def more(state):
            return (state[1] > 1e-3) & (state[0] < 60)

        def refine(state):
            x_ref[...] = x_ref[...] + mm_full(x_ref[...], e_ref[...])
            return (state[0] + 1, residual())

        lax.while_loop(more, refine, (jnp.int32(0), residual()))

    x_ref[...] = x_ref[...] + mm(x_ref[...].astype(bf16), e_ref[...].astype(bf16))


piece = 32
MESH = pl.DeviceIdType.MESH


def pieces_of(size):
    blocks = size // 128
    return [
        (row, column, part)
        for row in range(blocks)
        for column in range(row + 1)
        for part in range(128 // piece)
    ]


def spread_kernel(insts, times, g_ref, h_ref, all_ref, pack, landed, *sems):
    rs_send, rs_recv, z_send, z_recv, x_send, x_recv, s_send, s_recv = sems
    size = g_ref.shape[0]
    t, z = lax.axis_index("tm"), lax.axis_index("inst")
    pairs = times // 2
    spot, core = t // 2, t % 2
    sibling = t + 1 - 2 * core
    z_peers = [lax.rem(z + k, insts) for k in range(insts)]
    z_from = [lax.rem(z - k + insts, insts) for k in range(insts)]
    t_peers = [lax.rem(spot + j, pairs) * 2 + core for j in range(pairs)]
    t_from = [lax.rem(spot - j + pairs, pairs) * 2 + core for j in range(pairs)]

    barrier = pltpu.get_barrier_semaphore()
    others = [{"inst": p} for p in z_peers[1:]] + [{"tm": p} for p in t_peers[1:] + [sibling]]
    for other in others:
        pl.semaphore_signal(barrier, inc=1, device_id=other, device_id_type=MESH)

    places = pieces_of(size)
    per = len(places) // insts
    tail = per * piece
    for number, (row, column, part) in enumerate(places):
        pack[number // per, pl.ds((number % per) * piece, piece), :] = g_ref[
            pl.ds(row * 128 + part * piece, piece), pl.ds(column * 128, 128)
        ]
    for chunk in range(insts):
        pack[chunk, pl.ds(tail, 8), :] = jnp.zeros((8, 128), f32)
    for row in range(size // 128):
        pack[0, pl.ds(tail + row, 1), :] = h_ref[:, pl.ds(row * 128, 128)]
    pl.semaphore_wait(barrier, len(others))

    def remote(source, target, send, recv, device):
        return pltpu.make_async_remote_copy(
            src_ref=source, dst_ref=target, send_sem=send, recv_sem=recv,
            device_id=device, device_id_type=MESH,
        )

    sent = []

    def start(copy):
        copy.start()
        sent.append(copy)

    rs = [
        remote(pack.at[z_peers[k]], landed.at[k], rs_send.at[k], rs_recv.at[k], {"inst": z_peers[k]})
        for k in range(1, insts)
    ]
    for copy in rs:
        start(copy)
    for copy in rs:
        copy.wait_recv()
    total = pack[z]
    for k in range(1, insts):
        total = total + landed[k]
    all_ref[t, z] = total

    def along_z(k, chunk, peer):
        here = all_ref.at[t, chunk]
        return remote(here, here, z_send.at[k], z_recv.at[k], {"inst": peer})

    def along_x(j, q, step, chunk, peer):
        here = all_ref.at[step, chunk]
        return remote(here, here, x_send.at[j, q], x_recv.at[j, q], {"tm": peer})

    def to_sibling(j, q, step, chunk):
        here = all_ref.at[step, chunk]
        return remote(here, here, s_send.at[j, q], s_recv.at[j, q], {"tm": sibling})

    for k in range(1, insts):
        start(along_z(k, z, z_peers[k]))
    for q in range(insts + 1):
        if q < insts:
            chunk = z_from[q]
            if q > 0:
                along_z(q, chunk, z_peers[q]).wait_recv()
            for j in range(1, pairs):
                start(along_x(j, q, t, chunk, t_peers[j]))
            start(to_sibling(0, q, t, chunk))
        if q > 0:
            chunk = z_from[q - 1]
            for j in range(1, pairs):
                along_x(j, q - 1, t_from[j], chunk, t_peers[j]).wait_recv()
                start(to_sibling(j, q - 1, t_from[j], chunk))
    for q in range(insts):
        for j in range(pairs):
            source = t_from[j] + 1 - 2 * core
            to_sibling(j, q, source, z_from[q]).wait_recv()
    for copy in sent:
        copy.wait_send()


def spread(matrix, vector, insts, times):
    size = matrix.shape[0]
    rows = len(pieces_of(size)) // insts * piece + 8
    whole = pl.BlockSpec(memory_space=pltpu.VMEM)
    dma = pltpu.SemaphoreType.DMA
    pairs = times // 2
    return pl.pallas_call(
        functools.partial(spread_kernel, insts, times),
        out_shape=jax.ShapeDtypeStruct((times, insts, rows, 128), f32),
        in_specs=[whole, whole],
        out_specs=whole,
        scratch_shapes=[
            pltpu.VMEM((insts, rows, 128), f32), pltpu.VMEM((insts, rows, 128), f32),
            dma((insts,)), dma((insts,)), dma((insts,)), dma((insts,)),
            dma((pairs, insts)), dma((pairs, insts)), dma((pairs, insts)), dma((pairs, insts)),
        ],
        compiler_params=pltpu.CompilerParams(
            collective_id=0, has_side_effects=True, vmem_limit_bytes=48 * 1024 * 1024
        ),
    )(matrix, vector)


def unpack(g_ref, index, a_ref):
    size = a_ref.shape[0]
    places = pieces_of(size)
    per = len(places) // g_ref.shape[1]
    for number, (row, column, part) in enumerate(places):
        a_ref[pl.ds(row * 128 + part * piece, piece), pl.ds(column * 128, 128)] = g_ref[
            index, number // per, pl.ds((number % per) * piece, piece), :
        ]
    for row in range(size // 128):
        for column in range(row):
            below = a_ref[pl.ds(row * 128, 128), pl.ds(column * 128, 128)]
            a_ref[pl.ds(column * 128, 128), pl.ds(row * 128, 128)] = below.T
    rows = g_ref[index, 0, pl.ds(per * piece, 8), :]
    return jnp.concatenate([rows[row : row + 1] for row in range(size // 128)], axis=1)


def chain_kernel(
    own_ref, g_ref, frow_ref, qrow_ref,
    mean_ref, var_ref, smooth_ref,
    m_ref, lam_ref, y_ref, prior_row_ref, prior_col_ref, own_y_ref,
    a_ref, x_ref, e_ref, ah_ref, ident_ref, r_ref, pr_row_ref, pr_col_ref,
):
    steps, size = g_ref.shape[0], frow_ref.shape[1]
    own = own_ref[0]
    ident_ref[...] = jnp.where(eye_mask(size), f32(1.0), f32(0.0))
    frow = frow_ref[...]
    fcol = jnp.sum(ident_ref[...] * frow, axis=1, keepdims=True)
    sq_row = jnp.sqrt(qrow_ref[...])
    sq_col = jnp.sum(ident_ref[...] * sq_row, axis=1, keepdims=True)
    f2_row, f2_col = frow * frow, fcol * fcol
    prior_row_ref[...] = jnp.ones_like(prior_row_ref)
    prior_col_ref[...] = jnp.ones_like(prior_col_ref)

    def step(index, carry):
        @pl.when(index < steps)
        def _():
            before = jnp.maximum(index - 1, 0)
            moved = jnp.where(index > 0, m_ref[before] * (fcol * frow), 0.0)
            y = unpack(g_ref, index, a_ref) * sq_row
            lam = a_ref[...] * (sq_col * sq_row) + (ident_ref[...] - moved)

            @pl.when(index == 0)
            def _():
                y_ref[0] = y

            @pl.when(index > 0)
            def _():
                y_ref[index] = y + frow * vec_mat(y_ref[before], m_ref[before])
                prior_row_ref[...] = prior_row_ref[...] / (prior_row_ref[...] + f2_row)
                prior_col_ref[...] = prior_col_ref[...] / (prior_col_ref[...] + f2_col)

            @pl.when(index == own)
            def _():
                lam_ref[...] = lam
                pr_row_ref[...] = prior_row_ref[...]
                pr_col_ref[...] = prior_col_ref[...]
                own_y_ref[...] = y_ref[index]

            a_ref[...] = lam

        last = index >= steps - 1
        extra = jnp.where(last, f32(0.0), f32(1.0))

        @pl.when(index == steps)
        def _():
            a_ref[...] = lam_ref[...]
            prior_row_ref[...] = pr_row_ref[...]
            prior_col_ref[...] = pr_col_ref[...]

        row_scale = lax.rsqrt(prior_row_ref[...] + extra * f2_row)
        col_scale = lax.rsqrt(prior_col_ref[...] + extra * f2_col)
        diagonal = ident_ref[...] * (extra * f2_row)
        a_ref[...] = (a_ref[...] + diagonal) * (col_scale * row_scale)
        inverse(a_ref, x_ref, e_ref, ah_ref, r_ref, ident_ref)
        m_ref[index] = x_ref[...] * (col_scale * row_scale)
        return carry

    lax.fori_loop(0, steps + 1, step, 0)
    covariance = m_ref[steps]
    mean_ref[...] = sq_row * vec_mat(own_y_ref[...], covariance)
    diagonal = jnp.sum(ident_ref[...] * covariance, axis=0, keepdims=True)
    var_ref[...] = qrow_ref[...] * diagonal
    final = vec_mat(y_ref[steps - 1], m_ref[steps - 1])

    def back(count, later):
        index = steps - 2 - count
        return vec_mat(y_ref[index] + frow * later, m_ref[index])

    smooth_ref[...] = sq_row * lax.fori_loop(0, steps - 1 - own, back, final)


def chain(own, matrices, persistence, shock_var):
    steps, size = matrices.shape[0], persistence.shape[0]
    row = jax.ShapeDtypeStruct((1, size), f32)
    square = pltpu.VMEM((size, size), f32)
    half = pltpu.VMEM((size, size), bf16)
    flat = pltpu.VMEM((1, size), f32)
    tall = pltpu.VMEM((size, 1), f32)
    whole = pl.BlockSpec(memory_space=pltpu.VMEM)
    return pl.pallas_call(
        chain_kernel,
        out_shape=(row, row, row),
        in_specs=[pl.BlockSpec(memory_space=pltpu.SMEM)] + [whole] * 3,
        out_specs=(whole, whole, whole),
        scratch_shapes=[
            pltpu.VMEM((steps + 1, size, size), f32), square, pltpu.VMEM((steps, 1, size), f32),
            flat, tall, flat, square, square, square, half, square,
            pltpu.VMEM((8, 128), f32), flat, tall,
        ],
        compiler_params=pltpu.CompilerParams(vmem_limit_bytes=60 * 1024 * 1024),
    )(
        own, matrices, persistence[None, :], shock_var[None, :],
    )


def information_kernel(quotes_ref, present_ref, noise_ref, loadings_ref, matrix_ref, vector_ref):
    @pl.when(pl.program_id(0) == 0)
    def _():
        matrix_ref[...] = jnp.zeros_like(matrix_ref)
        vector_ref[...] = jnp.zeros_like(vector_ref)

    loadings = loadings_ref[...]
    scaled = present_ref[...].astype(f32) / noise_ref[...]
    weighted = (loadings.T.astype(f32) * scaled).astype(bf16)
    matrix_ref[...] += mm(weighted, loadings)
    quotes = quotes_ref[...]
    high = quotes.astype(bf16).astype(f32)
    rest = quotes - high
    middle = rest.astype(bf16).astype(f32)
    index = lax.broadcasted_iota(jnp.int32, (16, quotes.shape[1]), 0)
    rows = jnp.where(index == 0, high, jnp.where(index == 1, middle, 0.0))
    rows = jnp.where(index == 2, rest - middle, rows).astype(bf16)
    sums = lax.dot_general(rows, weighted, (((1,), (1,)), ((), ())), preferred_element_type=f32)
    vector_ref[...] += jnp.sum(sums, axis=0, keepdims=True)


def step_information(loadings, noise_var, quotes, present):
    insts, size = loadings.shape
    chunk = 1024 if insts % 1024 == 0 else 512
    flat = pl.BlockSpec((1, chunk), lambda i: (0, i))
    return pl.pallas_call(
        information_kernel,
        grid=(insts // chunk,),
        out_shape=(
            jax.ShapeDtypeStruct((size, size), f32), jax.ShapeDtypeStruct((1, size), f32),
        ),
        in_specs=[flat, flat, flat, pl.BlockSpec((chunk, size), lambda i: (i, 0))],
        out_specs=(
            pl.BlockSpec((size, size), lambda i: (0, 0)), pl.BlockSpec((1, size), lambda i: (0, 0)),
        ),
        compiler_params=pltpu.CompilerParams(vmem_limit_bytes=60 * 1024 * 1024),
    )(quotes, present, noise_var[None, :], loadings)


def body(quotes, present, loadings, noise_var, persistence, shock_var):
    parts = step_information(loadings, noise_var, quotes, present)
    matrices = spread(*parts, lax.axis_size("inst"), lax.axis_size("tm"))
    own = lax.axis_index("tm").astype(jnp.int32)[None]
    return chain(own, matrices, persistence, shock_var)


def solution(mesh):
    placed = (
        P(("group", "tm"), "inst"),
        P(("group", "tm"), "inst"),
        P("inst", None),
        P("inst"),
        P(),
        P(),
    )
    return jax.shard_map(
        body,
        mesh=mesh,
        in_specs=placed,
        out_specs=(P(("group", "tm"), None), P(("group", "tm"), None), P(("group", "tm"), None)),
        check_vma=False,
    )
```
